32 devices in a mesh: fsdp: 4 (over x, core), seq: 8 (over z, y).
Axes of the slice: x: 2, y: 2, z: 4, core: 2. Of those that a mesh axis runs over, the one named last changes fastest.
Arguments:
- tokens: bfloat16 [4, 56, 28, 512], P('fsdp', 'seq'), may hold values from -6 to 6
- cotangent: bfloat16 [4, 56, 28, 512], P('fsdp', 'seq'), may hold values from -6 to 6
- region_ids: int32 [56, 28], replicated, may hold values from 0 to 3
- relative_index: int32 [49, 49], replicated, may hold values from 0 to 168, as said below
- first_gain: bfloat16 [512], P('fsdp'), may hold values from 0.5 to 1.5
- first_offset: bfloat16 [512], P('fsdp'), may hold values from -3 to 3
- qkv_weight: bfloat16 [512, 1536], P('fsdp'), may hold values from -0.25 to 0.25
- proj_weight: bfloat16 [512, 512], P('fsdp'), may hold values from -0.75 to 0.75
- bias_table: bfloat16 [16, 169], P('fsdp'), may hold values from -4 to 4
- second_gain: bfloat16 [512], P('fsdp'), may hold values from 0.5 to 1.5
- second_offset: bfloat16 [512], P('fsdp'), may hold values from -3 to 3
- expand_weight: bfloat16 [512, 2048], P('fsdp'), may hold values from -0.25 to 0.25
- reduce_weight: bfloat16 [2048, 512], P('fsdp'), may hold values from -0.125 to 0.125
Outputs:
- output: bfloat16 [4, 56, 28, 512], P('fsdp', 'seq')
- tokens_grad: float32 [4, 56, 28, 512], P('fsdp', 'seq')
- first_gain_grad: float32 [512], P('fsdp')
- first_offset_grad: float32 [512], P('fsdp')
- qkv_weight_grad: float32 [512, 1536], P('fsdp')
- proj_weight_grad: float32 [512, 512], P('fsdp')
- bias_table_grad: float32 [16, 169], P('fsdp')
- second_gain_grad: float32 [512], P('fsdp')
- second_offset_grad: float32 [512], P('fsdp')
- expand_weight_grad: float32 [512, 2048], P('fsdp')
- reduce_weight_grad: float32 [2048, 512], P('fsdp')
The draws below stay inside these ranges and needn't reach their ends.
Inputs may be any that keep to these rules, and one draw needn't show every extreme that they name: relative_index[i, j] depends only on the row and column offsets between positions i and j of a 7 x 7 window, and distinct offsets give distinct entries.
All inputs are finite; a program needn't handle non-finite values.
Results may differ from the reference program's by a relative error of at most 0.018.
Values may be sent and summed in bfloat16 or wider, within the bound.
A program may use at most 128 MiB of HBM per device.

```python
import jax
import jax.numpy as jnp
from jax import lax

C = 512
NH = 16
FF = 2048
HD = 32
WS = 7
SHIFT = 3
RELS = 169
IMAGES = 4
HGT = 56
WID = 28


def draw_relative_index(key, part):
    labels = jax.random.permutation(key, (2 * WS - 1) ** 2).astype(jnp.int32)
    places = jnp.arange(WS * WS, dtype=jnp.int32)
    row_of = places // WS
    col_of = places % WS
    offsets = (row_of[:, None] - row_of[None, :] + WS - 1) * (2 * WS - 1) + (col_of[:, None] - col_of[None, :] + WS - 1)
    return labels[offsets].astype(jnp.int32)


def touch_ends(values, stream_key, smallest, largest):
    dims = values.shape
    spot = [jax.random.randint(jax.random.fold_in(stream_key, axis), (), 0, dims[axis]) for axis in range(len(dims))]
    values = values.at[tuple(spot)].set(smallest)
    longest = dims.index(max(dims))
    spot[longest] = (spot[longest] + 1) % dims[longest]
    return values.at[tuple(spot)].set(largest)


def level_of(own_key, shape, cuts, smallest, high):
    loudness, own = 1.0, jax.random.fold_in(own_key, 6)
    for axis_at, shards_of in cuts:
        steps = jnp.exp(jax.random.uniform(jax.random.fold_in(own, axis_at), (shards_of,), jnp.float32, smallest / len(cuts), high / len(cuts)))
        loudness = loudness * jnp.repeat(steps, shape[axis_at] // shards_of).reshape([-1 if axis == axis_at else 1 for axis in range(len(shape))])
    return loudness


def noise(own_key, dims, spread, limit, shards=(), kind=jnp.bfloat16):
    factor_of = level_of(own_key, dims, shards, -0.22, 0.18) if shards else 1.0
    values = jax.random.normal(own_key, dims, jnp.float32) * spread * factor_of
    return jnp.minimum(jnp.maximum(values, -limit), limit).astype(kind)


def setup_inputs(seed: int = 0) -> dict:
    streams_of = jax.random.split(jax.random.key(seed), 14)
    tokens = noise(streams_of[0], (IMAGES, HGT, WID, C), 1.0, 6.0, ((0, 4), (1, 8)))
    cotangent = noise(streams_of[1], (IMAGES, HGT, WID, C), 1.0, 6.0, ((0, 4), (1, 8)))
    region_ids = touch_ends(jax.random.randint(streams_of[2], (HGT, WID), 0, 4), jax.random.fold_in(streams_of[2], 1), 0, 3).astype(jnp.int32)
    relative_index = draw_relative_index(jax.random.fold_in(streams_of[13], 71), 0)
    first_gain = jnp.clip(1.0 + 0.1 * jax.random.normal(streams_of[4], (C,), jnp.float32), 0.5, 1.5).astype(jnp.bfloat16)
    first_offset = noise(streams_of[5], (C,), 0.5, 3.0, ((0, 4),))
    qkv_weight = noise(streams_of[6], (C, 3 * C), C ** -0.5, 0.25, ((0, 4),))
    proj_weight = noise(streams_of[7], (C, C), (C // 8) ** -0.5, 0.75, ((0, 4),))
    bias_table = noise(streams_of[8], (NH, RELS), 1.0, 4.0, ((0, 4),))
    second_gain = jnp.clip(1.0 + 0.1 * jax.random.normal(streams_of[9], (C,), jnp.float32), 0.5, 1.5).astype(jnp.bfloat16)
    second_offset = noise(streams_of[10], (C,), 0.5, 3.0, ((0, 4),))
    expand_weight = noise(streams_of[11], (C, FF), C ** -0.5, 0.25, ((0, 4),))
    reduce_weight = noise(streams_of[12], (FF, C), FF ** -0.5, 0.125, ((0, 4),))
    return {"tokens": tokens, "cotangent": cotangent, "region_ids": region_ids, "relative_index": relative_index, "first_gain": first_gain, "first_offset": first_offset, "qkv_weight": qkv_weight, "proj_weight": proj_weight, "bias_table": bias_table, "second_gain": second_gain, "second_offset": second_offset, "expand_weight": expand_weight, "reduce_weight": reduce_weight}


EPSILON = 1e-05
MASKED = -100.0
SQRT_HALF = 0.7071067811865476
INV_ROOT_TAU = 0.3989422804014327

def layer_norm(values, norm_gain, norm_offset):
    average = lax.optimization_barrier(jnp.mean(values, axis=-1, keepdims=True))
    centred = values - average
    variance = lax.optimization_barrier(jnp.mean(centred * centred, axis=-1, keepdims=True))
    inverse = lax.rsqrt(variance + EPSILON)
    normed = centred * inverse
    return (normed * norm_gain + norm_offset, normed, inverse)

def norm_back(upstream, normed, inverse, norm_gain):
    scaled = upstream * norm_gain
    mean_grad = lax.optimization_barrier(jnp.mean(scaled, axis=-1, keepdims=True))
    second = lax.optimization_barrier(jnp.mean(scaled * normed, axis=-1, keepdims=True))
    grad_in = inverse * (scaled - mean_grad - normed * second)
    lead_axes = tuple(range(upstream.ndim - 1))
    return (grad_in, lax.optimization_barrier(jnp.sum(upstream * normed, axis=lead_axes)), lax.optimization_barrier(jnp.sum(upstream, axis=lead_axes)))

def gelu_parts(hidden):
    normal_cdf = 0.5 * (1.0 + jax.scipy.special.erf(hidden * SQRT_HALF))
    density = jnp.exp(-0.5 * hidden * hidden) * INV_ROOT_TAU
    return (hidden * normal_cdf, normal_cdf + hidden * density)

def widen(low_array):
    return lax.optimization_barrier(low_array).astype(jnp.float32)

def tile_image(field_in):
    lead_count = field_in.shape[2]
    pieces = field_in.reshape(HGT // WS, WS, WID // WS, WS, lead_count, NH, HD)
    return pieces.transpose(4, 0, 2, 5, 1, 3, 6).reshape(lead_count, HGT // WS, WID // WS, NH, WS * WS, HD)

def untile_image(window_tiles):
    lead_count = window_tiles.shape[0]
    pieces = window_tiles.reshape(lead_count, HGT // WS, WID // WS, NH, WS, WS, HD)
    return pieces.transpose(1, 4, 2, 5, 0, 3, 6).reshape(HGT, WID, lead_count, C)

def reference(tokens, cotangent, region_ids, relative_index, first_gain, first_offset, qkv_weight, proj_weight, bias_table, second_gain, second_offset, expand_weight, reduce_weight):
    gain_one = first_gain.astype(jnp.float32)
    offset_one = first_offset.astype(jnp.float32)
    gain_two = second_gain.astype(jnp.float32)
    offset_two = second_offset.astype(jnp.float32)
    query_scale = HD ** (-0.5)
    factors = jnp.array([query_scale, 1.0, 1.0], dtype=jnp.float32)[:, None]
    rel_bias = bias_table.astype(jnp.float32)[:, relative_index]
    region_tiles = region_ids.reshape(HGT // WS, WS, WID // WS, WS).transpose(0, 2, 1, 3).reshape(HGT // WS, WID // WS, WS * WS)
    mask_add = jnp.where(region_tiles[..., :, None] == region_tiles[..., None, :], 0.0, MASKED).astype(jnp.float32)[:, :, None]

    def one_image(totals, items):
        image, image_cot = items
        inputs = image.astype(jnp.float32)
        normed_one, hat_one, inv_one = layer_norm(inputs, gain_one, offset_one)
        first_low = normed_one.astype(jnp.bfloat16).reshape(-1, C)
        qkv_all = jnp.dot(first_low, qkv_weight, preferred_element_type=jnp.float32).reshape(HGT, WID, 3, C)
        qkv_low = (qkv_all * factors).astype(jnp.bfloat16)
        qkv_tiles = widen(tile_image(jnp.roll(qkv_low, (-SHIFT, -SHIFT), axis=(0, 1))))
        queries, key_tiles, value_tiles = (qkv_tiles[0], qkv_tiles[1], qkv_tiles[2])
        scores = jnp.einsum('xyhid,xyhjd->xyhij', queries, key_tiles) + rel_bias + mask_add
        exp_scores = jnp.exp(scores)
        row_total = lax.optimization_barrier(jnp.sum(exp_scores, axis=-1, keepdims=True))
        log_total = jnp.log(row_total)
        attn_probs = widen((exp_scores / row_total).astype(jnp.bfloat16))
        attn_tiles = jnp.einsum('xyhij,xyhjd->xyhid', attn_probs, value_tiles).astype(jnp.bfloat16)
        attended = jnp.roll(untile_image(attn_tiles[None])[:, :, 0], (SHIFT, SHIFT), axis=(0, 1)).reshape(-1, C)
        middle = inputs + jnp.dot(attended, proj_weight, preferred_element_type=jnp.float32).reshape(HGT, WID, C)
        normed_two, hat_two, inv_two = layer_norm(middle, gain_two, offset_two)
        second_low = normed_two.astype(jnp.bfloat16).reshape(-1, C)
        hidden = jnp.dot(second_low, expand_weight, preferred_element_type=jnp.float32)
        activated, slope = gelu_parts(hidden)
        act_low = activated.astype(jnp.bfloat16)
        output = (middle + jnp.dot(act_low, reduce_weight, preferred_element_type=jnp.float32).reshape(HGT, WID, C)).astype(jnp.bfloat16)
        cot_flat = image_cot.reshape(-1, C)
        reduce_grad = jnp.dot(act_low.T, cot_flat, preferred_element_type=jnp.float32)
        hidden_grad = (jnp.dot(cot_flat, reduce_weight.T, preferred_element_type=jnp.float32) * slope).astype(jnp.bfloat16)
        expand_grad = jnp.dot(second_low.T, hidden_grad, preferred_element_type=jnp.float32)
        upstream_two = jnp.dot(hidden_grad, expand_weight.T, preferred_element_type=jnp.float32).reshape(HGT, WID, C)
        back_two, gain_two_grad, offset_two_grad = norm_back(upstream_two, hat_two, inv_two, gain_two)
        middle_grad = image_cot.astype(jnp.float32) + back_two
        middle_low = middle_grad.astype(jnp.bfloat16).reshape(-1, C)
        proj_grad = jnp.dot(attended.T, middle_low, preferred_element_type=jnp.float32)
        attended_grad = jnp.dot(middle_low, proj_weight.T, preferred_element_type=jnp.float32).astype(jnp.bfloat16).reshape(HGT, WID, 1, C)
        grad_tiles = widen(tile_image(jnp.roll(attended_grad, (-SHIFT, -SHIFT), axis=(0, 1))))[0]
        probs_back = jnp.exp(scores - log_total)
        probs_low = widen(probs_back.astype(jnp.bfloat16))
        value_grad = jnp.einsum('xyhij,xyhid->xyhjd', probs_low, grad_tiles)
        prob_grad = jnp.einsum('xyhid,xyhjd->xyhij', grad_tiles, value_tiles)
        score_grad = probs_back * (prob_grad - lax.optimization_barrier(jnp.sum(probs_back * prob_grad, axis=-1, keepdims=True)))
        score_low = widen(score_grad.astype(jnp.bfloat16))
        query_grad = jnp.einsum('xyhij,xyhjd->xyhid', score_low, key_tiles) * query_scale
        key_grad = jnp.einsum('xyhij,xyhid->xyhjd', score_low, queries)
        stacked = jnp.stack([query_grad, key_grad, value_grad]).astype(jnp.bfloat16)
        qkv_grad = jnp.roll(untile_image(stacked), (SHIFT, SHIFT), axis=(0, 1)).reshape(-1, 3 * C)
        qkv_grad_w = jnp.dot(first_low.T, qkv_grad, preferred_element_type=jnp.float32)
        upstream_one = jnp.dot(qkv_grad, qkv_weight.T, preferred_element_type=jnp.float32).reshape(HGT, WID, C)
        back_one, gain_one_grad, offset_one_grad = norm_back(upstream_one, hat_one, inv_one, gain_one)
        tokens_grad = middle_grad + back_one
        score_sum = lax.optimization_barrier(jnp.sum(score_grad, axis=(0, 1))).reshape(NH, -1)
        table_grad = jax.ops.segment_sum(score_sum.T, relative_index.reshape(-1), num_segments=RELS).T
        terms = (gain_one_grad, offset_one_grad, qkv_grad_w, proj_grad, table_grad, gain_two_grad, offset_two_grad, expand_grad, reduce_grad)
        return (tuple((total + term for total, term in zip(totals, terms))), (output, tokens_grad))
    start = (jnp.zeros((C,), jnp.float32), jnp.zeros((C,), jnp.float32), jnp.zeros((C, 3 * C), jnp.float32), jnp.zeros((C, C), jnp.float32), jnp.zeros((NH, RELS), jnp.float32), jnp.zeros((C,), jnp.float32), jnp.zeros((C,), jnp.float32), jnp.zeros((C, FF), jnp.float32), jnp.zeros((FF, C), jnp.float32))
    sums, per_image = lax.scan(one_image, start, (tokens, cotangent))
    outputs, grads_in = per_image
    return (outputs, grads_in, sums[0], sums[1], sums[2], sums[3], sums[4], sums[5], sums[6], sums[7], sums[8])
```

```python
import jax
import jax.numpy as jnp
from jax import lax
from jax.sharding import PartitionSpec as P

WS = 7
SHIFT = 3


EPSILON = 1e-05
MASKED = -100.0
SQRT_HALF = 0.7071067811865476
INV_ROOT_TAU = 0.3989422804014327


def layer_norm(values, norm_gain, norm_offset):
    average = jnp.mean(values, axis=-1, keepdims=True)
    centred = values - average
    variance = jnp.mean(centred * centred, axis=-1, keepdims=True)
    inverse = lax.rsqrt(variance + EPSILON)
    normed = centred * inverse
    return (normed * norm_gain + norm_offset, normed, inverse)


def norm_back(upstream, normed, inverse, norm_gain):
    scaled = upstream * norm_gain
    mean_grad = jnp.mean(scaled, axis=-1, keepdims=True)
    second = jnp.mean(scaled * normed, axis=-1, keepdims=True)
    grad_in = inverse * (scaled - mean_grad - normed * second)
    lead_axes = tuple(range(upstream.ndim - 1))
    return (grad_in, jnp.sum(upstream * normed, axis=lead_axes), jnp.sum(upstream, axis=lead_axes))


def gelu_parts(hidden):
    normal_cdf = 0.5 * (1.0 + jax.scipy.special.erf(hidden * SQRT_HALF))
    density = jnp.exp(-0.5 * hidden * hidden) * INV_ROOT_TAU
    return (hidden * normal_cdf, normal_cdf + hidden * density)


def to_windows(field_in):
    num_rows, num_cols, width = field_in.shape
    pieces = field_in.reshape(num_rows // WS, WS, num_cols // WS, WS, width)
    return pieces.transpose(0, 2, 1, 3, 4).reshape(-1, WS * WS, width)


def from_windows(tiles, num_rows, num_cols):
    pieces = tiles.reshape(num_rows // WS, num_cols // WS, WS, WS, tiles.shape[-1])
    return pieces.transpose(0, 2, 1, 3, 4).reshape(num_rows, num_cols, tiles.shape[-1])


def make_mask(regions):
    num_rows, num_cols = regions.shape
    region_tiles = (
        regions.reshape(num_rows // WS, WS, num_cols // WS, WS)
        .transpose(0, 2, 1, 3)
        .reshape(-1, WS * WS)
    )
    same_region = region_tiles[..., :, None] == region_tiles[..., None, :]
    return jnp.where(same_region, 0.0, MASKED).astype(jnp.float32)


def one_hot_index(relative_index, entries):
    return (relative_index[..., None] == jnp.arange(entries, dtype=jnp.int32)).astype(jnp.bfloat16)


def table_bias(table_low, relative_index):
    onehot = one_hot_index(relative_index, table_low.shape[-1])
    return jnp.einsum("ijr,hr->hij", onehot, table_low, preferred_element_type=jnp.float32)


def table_grad(bias_grad, relative_index, entries):
    onehot = one_hot_index(relative_index, entries).astype(jnp.float32)
    return jnp.einsum("hij,ijr->hr", bias_grad, onehot, precision=lax.Precision.HIGHEST)


def split_heads(tiles, num_heads):
    return tiles.reshape(tiles.shape[0], tiles.shape[1], num_heads, -1).transpose(0, 2, 1, 3)


def join_heads(tiles):
    count, num_heads, positions, head_dim = tiles.shape
    return tiles.transpose(0, 2, 1, 3).reshape(count, positions, num_heads * head_dim)


def mm(form, left, right):
    return jnp.einsum(form, left, right, preferred_element_type=jnp.float32)


def shifted_rows(field, size):
    ring = [(at, (at - 1) % size) for at in range(size)]
    later = lax.ppermute(field[:SHIFT], "seq", ring)
    return jnp.roll(jnp.concatenate([field[SHIFT:], later], axis=0), -SHIFT, axis=1)


def unshifted_rows(field, size):
    ring = [(at, (at + 1) % size) for at in range(size)]
    field = jnp.roll(field, SHIFT, axis=1)
    keep = field.shape[0] - SHIFT
    earlier = lax.ppermute(field[keep:], "seq", ring)
    return jnp.concatenate([earlier, field[:keep]], axis=0)


def shards(
    tokens,
    cotangent,
    region_ids,
    relative_index,
    first_gain,
    first_offset,
    qkv_weight,
    proj_weight,
    bias_table,
    second_gain,
    second_offset,
    expand_weight,
    reduce_weight,
):
    owners = lax.axis_size("fsdp")
    size = lax.axis_size("seq")
    part = first_gain.shape[0]
    small = jnp.concatenate(
        [first_gain, first_offset, second_gain, second_offset, bias_table.reshape(-1)]
    )
    small_full = lax.all_gather(small, "fsdp", axis=0, tiled=False)
    vectors = [
        small_full[:, at * part : (at + 1) * part].reshape(-1).astype(jnp.float32)
        for at in range(4)
    ]
    gain_one, offset_one, gain_two, offset_two = vectors
    table_rows, entries = bias_table.shape
    table_full = small_full[:, 4 * part :].reshape(-1, entries)
    qkv_full = lax.all_gather(qkv_weight, "fsdp", axis=0, tiled=True)
    proj_full = lax.all_gather(proj_weight, "fsdp", axis=0, tiled=True)
    expand_full = lax.all_gather(expand_weight, "fsdp", axis=0, tiled=True)
    reduce_full = lax.all_gather(reduce_weight, "fsdp", axis=0, tiled=True)
    _, num_rows, num_cols, width = tokens.shape
    num_heads = table_full.shape[0]
    query_scale = (width // num_heads) ** (-0.5)

    image_low = to_windows(shifted_rows(tokens[0], size))
    cot = to_windows(shifted_rows(cotangent[0], size))
    inputs = image_low.astype(jnp.float32)
    rel_bias = table_bias(table_full, relative_index)
    regions = lax.dynamic_slice_in_dim(
        region_ids, lax.axis_index("seq") * num_rows, num_rows, 0
    )
    mask_add = make_mask(regions)

    normed_one, hat_one, inv_one = layer_norm(inputs, gain_one, offset_one)
    first_low = normed_one.astype(jnp.bfloat16)
    factors = jnp.concatenate(
        [jnp.full((width,), query_scale, jnp.float32), jnp.ones((2 * width,), jnp.float32)]
    )
    qkv = (mm("wic,cd->wid", first_low, qkv_full) * factors).astype(jnp.bfloat16)
    queries = split_heads(qkv[..., :width], num_heads)
    keys = split_heads(qkv[..., width : 2 * width], num_heads)
    values = split_heads(qkv[..., 2 * width :], num_heads)
    scores = mm("whid,whjd->whij", queries, keys) + rel_bias + mask_add[:, None]
    exp_scores = jnp.exp(scores)
    row_total = jnp.sum(exp_scores, axis=-1, keepdims=True)
    probs = exp_scores / row_total
    probs_low = probs.astype(jnp.bfloat16)
    attended = join_heads(mm("whij,whjd->whid", probs_low, values).astype(jnp.bfloat16))

    middle = inputs + mm("wic,cd->wid", attended, proj_full)
    normed_two, hat_two, inv_two = layer_norm(middle, gain_two, offset_two)
    second_low = normed_two.astype(jnp.bfloat16)
    hidden = mm("wic,cf->wif", second_low, expand_full)
    activated, slope = gelu_parts(hidden)
    act_low = activated.astype(jnp.bfloat16)
    out_tiles = (middle + mm("wif,fc->wic", act_low, reduce_full)).astype(jnp.bfloat16)
    output = unshifted_rows(from_windows(out_tiles, num_rows, num_cols), size)[None]

    def to_owner(grad):
        share = lax.psum_scatter(
            grad.astype(jnp.bfloat16), "fsdp", scatter_dimension=0, tiled=True
        )
        return lax.psum(share, "seq")

    reduce_total = to_owner(mm("wif,wic->fc", act_low, cot))
    hidden_grad = (mm("wic,fc->wif", cot, reduce_full) * slope).astype(jnp.bfloat16)
    expand_total = to_owner(mm("wic,wif->cf", second_low, hidden_grad))
    upstream_two = mm("wif,cf->wic", hidden_grad, expand_full)
    back_two, gain_two_grad, offset_two_grad = norm_back(upstream_two, hat_two, inv_two, gain_two)
    middle_grad = cot.astype(jnp.float32) + back_two
    middle_low = middle_grad.astype(jnp.bfloat16)
    proj_grad = mm("wic,wid->cd", attended, middle_low)

    attended_grad = mm("wid,cd->wic", middle_low, proj_full).astype(jnp.bfloat16)
    grad_tiles = split_heads(attended_grad, num_heads)
    value_grad = mm("whij,whid->whjd", probs_low, grad_tiles)
    prob_grad = mm("whid,whjd->whij", grad_tiles, values)
    score_grad = probs * (prob_grad - jnp.sum(probs * prob_grad, axis=-1, keepdims=True))
    score_low = score_grad.astype(jnp.bfloat16)
    query_grad = mm("whij,whjd->whid", score_low, keys) * query_scale
    key_grad = mm("whij,whid->whjd", score_low, queries)
    qkv_grad = jnp.concatenate(
        [join_heads(grad.astype(jnp.bfloat16)) for grad in (query_grad, key_grad, value_grad)],
        axis=-1,
    )
    table_part = table_grad(jnp.sum(score_grad, axis=0), relative_index, entries)
    qkv_grad_w = mm("wic,wid->cd", first_low, qkv_grad)
    upstream_one = mm("wid,cd->wic", qkv_grad, qkv_full)
    back_one, gain_one_grad, offset_one_grad = norm_back(upstream_one, hat_one, inv_one, gain_one)
    grad_in = from_windows(middle_grad + back_one, num_rows, num_cols)
    tokens_grad = unshifted_rows(grad_in, size)[None]

    small_grads = jnp.concatenate(
        [
            grad.reshape(owners, -1)
            for grad in (gain_one_grad, offset_one_grad, gain_two_grad, offset_two_grad, table_part)
        ],
        axis=1,
    )
    qkv_total = to_owner(qkv_grad_w)
    proj_total = to_owner(proj_grad)
    small_total = lax.psum(small_grads, ("fsdp", "seq"))
    small_total = lax.dynamic_slice_in_dim(small_total, lax.axis_index("fsdp"), 1, 0)[0]
    own = [small_total[at * part : (at + 1) * part] for at in range(4)]
    table_total = small_total[4 * part :].reshape(table_rows, entries)
    wide = jnp.float32
    return (
        output,
        tokens_grad,
        own[0],
        own[1],
        qkv_total.astype(wide),
        proj_total.astype(wide),
        table_total,
        own[2],
        own[3],
        expand_total.astype(wide),
        reduce_total.astype(wide),
    )


def solution(mesh):
    placed = (
        P("fsdp", "seq", None, None),
        P("fsdp", "seq", None, None),
        P(),
        P(),
        P("fsdp"),
        P("fsdp"),
        P("fsdp", None),
        P("fsdp", None),
        P("fsdp", None),
        P("fsdp"),
        P("fsdp"),
        P("fsdp", None),
        P("fsdp", None),
    )
    return jax.shard_map(
        shards,
        mesh=mesh,
        in_specs=placed,
        out_specs=(
            P("fsdp", "seq", None, None),
            P("fsdp", "seq", None, None),
            P("fsdp"),
            P("fsdp"),
            P("fsdp", None),
            P("fsdp", None),
            P("fsdp", None),
            P("fsdp"),
            P("fsdp"),
            P("fsdp", None),
            P("fsdp", None),
        ),
        check_vma=False,
    )
```

```python
import functools

import jax
import jax.numpy as jnp
from jax import lax
from jax.experimental import pallas as pl
from jax.experimental.pallas import tpu as pltpu
from jax.sharding import PartitionSpec as P

WS = 7
SHIFT = 3


EPSILON = 1e-05
MASKED = -100.0
SQRT_HALF = 0.7071067811865476
INV_ROOT_TAU = 0.3989422804014327


def layer_norm(values, norm_gain, norm_offset):
    average = jnp.mean(values, axis=-1, keepdims=True)
    centred = values - average
    variance = jnp.mean(centred * centred, axis=-1, keepdims=True)
    inverse = lax.rsqrt(variance + EPSILON)
    normed = centred * inverse
    return (normed * norm_gain + norm_offset, normed, inverse)


def norm_back(upstream, normed, inverse, norm_gain):
    scaled = upstream * norm_gain
    mean_grad = jnp.mean(scaled, axis=-1, keepdims=True)
    second = jnp.mean(scaled * normed, axis=-1, keepdims=True)
    grad_in = inverse * (scaled - mean_grad - normed * second)
    lead_axes = tuple(range(upstream.ndim - 1))
    return (grad_in, jnp.sum(upstream * normed, axis=lead_axes), jnp.sum(upstream, axis=lead_axes))


def gelu_parts(hidden):
    normal_cdf = 0.5 * (1.0 + jax.scipy.special.erf(hidden * SQRT_HALF))
    density = jnp.exp(-0.5 * hidden * hidden) * INV_ROOT_TAU
    return (hidden * normal_cdf, normal_cdf + hidden * density)


def to_windows(field_in):
    num_rows, num_cols, width = field_in.shape
    pieces = field_in.reshape(num_rows // WS, WS, num_cols // WS, WS, width)
    return pieces.transpose(0, 2, 1, 3, 4).reshape(-1, WS * WS, width)


def from_windows(tiles, num_rows, num_cols):
    pieces = tiles.reshape(num_rows // WS, num_cols // WS, WS, WS, tiles.shape[-1])
    return pieces.transpose(0, 2, 1, 3, 4).reshape(num_rows, num_cols, tiles.shape[-1])


def make_mask(regions):
    num_rows, num_cols = regions.shape
    region_tiles = (
        regions.reshape(num_rows // WS, WS, num_cols // WS, WS)
        .transpose(0, 2, 1, 3)
        .reshape(-1, WS * WS)
    )
    same_region = region_tiles[..., :, None] == region_tiles[..., None, :]
    return jnp.where(same_region, 0.0, MASKED).astype(jnp.float32)


def one_hot_index(relative_index, entries):
    return (relative_index[..., None] == jnp.arange(entries, dtype=jnp.int32)).astype(jnp.bfloat16)


def table_bias(table_low, relative_index):
    onehot = one_hot_index(relative_index, table_low.shape[-1])
    return jnp.einsum("ijr,hr->hij", onehot, table_low, preferred_element_type=jnp.float32)


def table_grad(bias_grad, relative_index, entries):
    onehot = one_hot_index(relative_index, entries).astype(jnp.float32)
    return jnp.einsum("hij,ijr->hr", bias_grad, onehot, precision=lax.Precision.HIGHEST)


def split_heads(tiles, num_heads):
    return tiles.reshape(tiles.shape[0], tiles.shape[1], num_heads, -1).transpose(0, 2, 1, 3)


def join_heads(tiles):
    count, num_heads, positions, head_dim = tiles.shape
    return tiles.transpose(0, 2, 1, 3).reshape(count, positions, num_heads * head_dim)


def mm(form, left, right):
    return jnp.einsum(form, left, right, preferred_element_type=jnp.float32)


def reduce_kernel(count, pairs, halves, *refs):
    grads, outs = refs[:count], refs[count : 2 * count]
    rest = refs[2 * count :]
    stages = [rest[at * count : (at + 1) * count] for at in range(7)]
    first_in, first_sum, second_in, second_sum, third_in, third_sum, fourth_in = stages
    send_sem, recv_sem = rest[7 * count :]
    place, line = lax.axis_index("fsdp"), lax.axis_index("seq")
    pair, core = place // 2, place % 2
    half, side = line // 2, line % 2
    mesh_id = pl.DeviceIdType.MESH

    def on_fsdp(pair_at, core_at):
        return {"fsdp": pair_at * 2 + core_at, "seq": line}

    def on_seq(half_at, side_at):
        return {"fsdp": place, "seq": half_at * 2 + side_at}

    pair_peers = [(pair + step) % pairs for step in range(1, pairs)]
    half_peers = [(half + step) % halves for step in range(1, halves)]
    everyone = [on_fsdp(pair, 1 - core)] + [on_fsdp(peer, core) for peer in pair_peers]
    everyone += [on_seq(half, 1 - side)] + [on_seq(peer, side) for peer in half_peers]
    barrier = pltpu.get_barrier_semaphore()
    for device in everyone:
        pl.semaphore_signal(barrier, inc=1, device_id=device, device_id_type=mesh_id)
    pl.semaphore_wait(barrier, len(everyone))

    started = {}
    used = [0] * count

    def send(stage, at, source, target, device):
        slot = used[at]
        used[at] += 1
        copy = pltpu.make_async_remote_copy(
            src_ref=source,
            dst_ref=target,
            send_sem=send_sem.at[at, slot],
            recv_sem=recv_sem.at[at, slot],
            device_id=device,
            device_id_type=mesh_id,
        )
        copy.start()
        started.setdefault((stage, at), []).append(copy)

    def arrived(stage, at):
        for copy in started[(stage, at)]:
            copy.wait_recv()

    def add(target, terms, low):
        total = terms[0].astype(jnp.float32)
        for term in terms[1:]:
            total = total + term.astype(jnp.float32)
        target[low] = total.astype(target.dtype)

    def sum_pair(at, pair_at):
        @pl.loop(0, 2 * halves)
        def _(piece):
            mine = grads[at][pair_at, core, piece // 2, piece % 2]
            came = first_in[at][pair_at, piece // 2, piece % 2]
            add(first_sum[at], [mine, came], (pair_at, piece // 2, piece % 2))

    def sum_side(at, side_at):
        @pl.loop(0, halves)
        def _(piece):
            terms = [first_sum[at][pair, piece, side_at]]
            terms += [second_in[at][step, piece, side_at] for step in range(pairs - 1)]
            add(second_sum[at], terms, (piece, side_at))

    def stage_first(at):
        send(0, at, grads[at].at[:, 1 - core], first_in[at], on_fsdp(pair, 1 - core))

    def stage_second(at):
        arrived(0, at)
        for step, peer in enumerate(pair_peers):
            sum_pair(at, peer)
            send(1, at, first_sum[at].at[peer], second_in[at].at[step], on_fsdp(peer, core))
        sum_pair(at, pair)

    def stage_third(at):
        arrived(1, at)
        sum_side(at, 1 - side)
        send(2, at, second_sum[at].at[:, 1 - side], third_in[at], on_seq(half, 1 - side))
        sum_side(at, side)

    def stage_fourth(at):
        arrived(2, at)

        @pl.loop(0, halves)
        def _(piece):
            add(third_sum[at], [second_sum[at][piece, side], third_in[at][piece]], (piece,))

        for step, peer in enumerate(half_peers):
            send(3, at, third_sum[at].at[peer], fourth_in[at].at[step], on_seq(peer, side))

    def stage_fifth(at):
        arrived(3, at)
        terms = [third_sum[at][half]] + [fourth_in[at][step] for step in range(halves - 1)]
        add(outs[at], terms, (half, side))
        own = outs[at].at[half, side]
        for peer in half_peers:
            send(4, at, own, own, on_seq(peer, side))

    def stage_sixth(at):
        arrived(4, at)
        own = outs[at].at[:, side]
        send(5, at, own, own, on_seq(half, 1 - side))

    for at in range(count):
        stage_first(at)
    later = (stage_second, stage_third, stage_fourth, stage_fifth, stage_sixth)
    for tick in range(count + len(later) - 1):
        for lag, stage in enumerate(later):
            if 0 <= tick - lag < count:
                stage(tick - lag)
    for at in range(count):
        arrived(5, at)
    for copies in started.values():
        for copy in copies:
            copy.wait_send()


def reduce_all(grads, owners, size):
    pairs, halves, count = owners // 2, size // 2, len(grads)
    blocks, shapes = [], []
    for grad in grads:
        rows, columns = grad.shape[0] // (owners * size), grad.shape[1]
        if rows % 16:
            rows, columns = rows * columns // 128, 128
        shapes.append((rows, columns))
        blocks.append(grad.reshape(pairs, 2, halves, 2, rows, columns))
    leads = [
        (pairs, halves, 2),
        (pairs, halves, 2),
        (max(pairs - 1, 1), halves, 2),
        (halves, 2),
        (halves,),
        (halves,),
        (max(halves - 1, 1),),
    ]
    scratch = [pltpu.VMEM(lead + shape, jnp.bfloat16) for lead in leads for shape in shapes]
    copies = 3 + (pairs - 1) + 2 * (halves - 1)
    sems = [pltpu.SemaphoreType.DMA((count, copies))] * 2
    totals = pl.pallas_call(
        functools.partial(reduce_kernel, count, pairs, halves),
        out_shape=[jax.ShapeDtypeStruct((halves, 2) + shape, jnp.bfloat16) for shape in shapes],
        in_specs=[pl.BlockSpec(memory_space=pltpu.VMEM)] * count,
        out_specs=[pl.BlockSpec(memory_space=pltpu.VMEM)] * count,
        scratch_shapes=scratch + sems,
        compiler_params=pltpu.CompilerParams(collective_id=0, has_side_effects=True),
    )(*blocks)
    return [
        total.reshape(grad.shape[0] // owners, grad.shape[1]) for total, grad in zip(totals, grads)
    ]


def shifted_rows(field, size):
    ring = [(at, (at - 1) % size) for at in range(size)]
    later = lax.ppermute(field[:SHIFT], "seq", ring)
    return jnp.roll(jnp.concatenate([field[SHIFT:], later], axis=0), -SHIFT, axis=1)


def unshifted_rows(field, size):
    ring = [(at, (at + 1) % size) for at in range(size)]
    field = jnp.roll(field, SHIFT, axis=1)
    keep = field.shape[0] - SHIFT
    earlier = lax.ppermute(field[keep:], "seq", ring)
    return jnp.concatenate([earlier, field[:keep]], axis=0)


def shards(
    tokens,
    cotangent,
    region_ids,
    relative_index,
    first_gain,
    first_offset,
    qkv_weight,
    proj_weight,
    bias_table,
    second_gain,
    second_offset,
    expand_weight,
    reduce_weight,
):
    owners = lax.axis_size("fsdp")
    size = lax.axis_size("seq")
    part = first_gain.shape[0]
    small = jnp.concatenate(
        [first_gain, first_offset, second_gain, second_offset, bias_table.reshape(-1)]
    )
    small_full = lax.all_gather(small, "fsdp", axis=0, tiled=False)
    vectors = [
        small_full[:, at * part : (at + 1) * part].reshape(-1).astype(jnp.float32)
        for at in range(4)
    ]
    gain_one, offset_one, gain_two, offset_two = vectors
    table_rows, entries = bias_table.shape
    table_full = small_full[:, 4 * part :].reshape(-1, entries)
    qkv_full = lax.all_gather(qkv_weight, "fsdp", axis=0, tiled=True)
    proj_full = lax.all_gather(proj_weight, "fsdp", axis=0, tiled=True)
    expand_full = lax.all_gather(expand_weight, "fsdp", axis=0, tiled=True)
    reduce_full = lax.all_gather(reduce_weight, "fsdp", axis=0, tiled=True)
    _, num_rows, num_cols, width = tokens.shape
    num_heads = table_full.shape[0]
    query_scale = (width // num_heads) ** (-0.5)

    image_low = to_windows(shifted_rows(tokens[0], size))
    cot = to_windows(shifted_rows(cotangent[0], size))
    inputs = image_low.astype(jnp.float32)
    rel_bias = table_bias(table_full, relative_index)
    regions = lax.dynamic_slice_in_dim(
        region_ids, lax.axis_index("seq") * num_rows, num_rows, 0
    )
    mask_add = make_mask(regions)

    normed_one, hat_one, inv_one = layer_norm(inputs, gain_one, offset_one)
    first_low = normed_one.astype(jnp.bfloat16)
    factors = jnp.concatenate(
        [jnp.full((width,), query_scale, jnp.float32), jnp.ones((2 * width,), jnp.float32)]
    )
    qkv = (mm("wic,cd->wid", first_low, qkv_full) * factors).astype(jnp.bfloat16)
    queries = split_heads(qkv[..., :width], num_heads)
    keys = split_heads(qkv[..., width : 2 * width], num_heads)
    values = split_heads(qkv[..., 2 * width :], num_heads)
    scores = mm("whid,whjd->whij", queries, keys) + rel_bias + mask_add[:, None]
    exp_scores = jnp.exp(scores)
    row_total = jnp.sum(exp_scores, axis=-1, keepdims=True)
    probs = exp_scores / row_total
    probs_low = probs.astype(jnp.bfloat16)
    attended = join_heads(mm("whij,whjd->whid", probs_low, values).astype(jnp.bfloat16))

    middle = inputs + mm("wic,cd->wid", attended, proj_full)
    normed_two, hat_two, inv_two = layer_norm(middle, gain_two, offset_two)
    second_low = normed_two.astype(jnp.bfloat16)
    hidden = mm("wic,cf->wif", second_low, expand_full)
    activated, slope = gelu_parts(hidden)
    act_low = activated.astype(jnp.bfloat16)
    out_tiles = (middle + mm("wif,fc->wic", act_low, reduce_full)).astype(jnp.bfloat16)
    output = unshifted_rows(from_windows(out_tiles, num_rows, num_cols), size)[None]

    reduce_grad = mm("wif,wic->fc", act_low, cot)
    hidden_grad = (mm("wic,fc->wif", cot, reduce_full) * slope).astype(jnp.bfloat16)
    expand_grad = mm("wic,wif->cf", second_low, hidden_grad)
    upstream_two = mm("wif,cf->wic", hidden_grad, expand_full)
    back_two, gain_two_grad, offset_two_grad = norm_back(upstream_two, hat_two, inv_two, gain_two)
    middle_grad = cot.astype(jnp.float32) + back_two
    middle_low = middle_grad.astype(jnp.bfloat16)
    proj_grad = mm("wic,wid->cd", attended, middle_low)

    attended_grad = mm("wid,cd->wic", middle_low, proj_full).astype(jnp.bfloat16)
    grad_tiles = split_heads(attended_grad, num_heads)
    value_grad = mm("whij,whid->whjd", probs_low, grad_tiles)
    prob_grad = mm("whid,whjd->whij", grad_tiles, values)
    score_grad = probs * (prob_grad - jnp.sum(probs * prob_grad, axis=-1, keepdims=True))
    score_low = score_grad.astype(jnp.bfloat16)
    query_grad = mm("whij,whjd->whid", score_low, keys) * query_scale
    key_grad = mm("whij,whid->whjd", score_low, queries)
    qkv_grad = jnp.concatenate(
        [join_heads(grad.astype(jnp.bfloat16)) for grad in (query_grad, key_grad, value_grad)],
        axis=-1,
    )
    table_part = table_grad(jnp.sum(score_grad, axis=0), relative_index, entries)
    qkv_grad_w = mm("wic,wid->cd", first_low, qkv_grad)
    upstream_one = mm("wid,cd->wic", qkv_grad, qkv_full)
    back_one, gain_one_grad, offset_one_grad = norm_back(upstream_one, hat_one, inv_one, gain_one)
    grad_in = from_windows(middle_grad + back_one, num_rows, num_cols)
    tokens_grad = unshifted_rows(grad_in, size)[None]

    small_grads = jnp.concatenate(
        [
            grad.reshape(owners, -1)
            for grad in (gain_one_grad, offset_one_grad, gain_two_grad, offset_two_grad, table_part)
        ],
        axis=1,
    )
    step = size * 16 * 128
    extra = -small_grads.shape[1] % step
    small_grads = jnp.pad(small_grads, ((0, 0), (0, extra))).reshape(-1, 128)
    wanted = (expand_grad, reduce_grad, qkv_grad_w, proj_grad, small_grads)
    expand_total, reduce_total, qkv_total, proj_total, small_total = reduce_all(
        [grad.astype(jnp.bfloat16) for grad in wanted], owners, size
    )
    small_total = small_total.reshape(-1).astype(jnp.float32)
    own = [small_total[at * part : (at + 1) * part] for at in range(4)]
    table_total = small_total[4 * part : 4 * part + table_rows * entries].reshape(table_rows, entries)
    wide = jnp.float32
    return (
        output,
        tokens_grad,
        own[0],
        own[1],
        qkv_total.astype(wide),
        proj_total.astype(wide),
        table_total,
        own[2],
        own[3],
        expand_total.astype(wide),
        reduce_total.astype(wide),
    )


def solution(mesh):
    placed = (
        P("fsdp", "seq", None, None),
        P("fsdp", "seq", None, None),
        P(),
        P(),
        P("fsdp"),
        P("fsdp"),
        P("fsdp", None),
        P("fsdp", None),
        P("fsdp", None),
        P("fsdp"),
        P("fsdp"),
        P("fsdp", None),
        P("fsdp", None),
    )
    return jax.shard_map(
        shards,
        mesh=mesh,
        in_specs=placed,
        out_specs=(
            P("fsdp", "seq", None, None),
            P("fsdp", "seq", None, None),
            P("fsdp"),
            P("fsdp"),
            P("fsdp", None),
            P("fsdp", None),
            P("fsdp", None),
            P("fsdp"),
            P("fsdp"),
            P("fsdp", None),
            P("fsdp", None),
        ),
        check_vma=False,
    )
```

```python
import functools

import jax
import jax.numpy as jnp
from jax import lax
from jax.experimental import pallas as pl
from jax.experimental.pallas import tpu as pltpu
from jax.sharding import PartitionSpec as P

WS = 7
SHIFT = 3


EPSILON = 1e-05
MASKED = -100.0
SQRT_HALF = 0.7071067811865476
INV_ROOT_TAU = 0.3989422804014327


def layer_norm(values, norm_gain, norm_offset):
    average = jnp.mean(values, axis=-1, keepdims=True)
    centred = values - average
    variance = jnp.mean(centred * centred, axis=-1, keepdims=True)
    inverse = lax.rsqrt(variance + EPSILON)
    normed = centred * inverse
    return (normed * norm_gain + norm_offset, normed, inverse)


def norm_back(upstream, normed, inverse, norm_gain):
    scaled = upstream * norm_gain
    mean_grad = jnp.mean(scaled, axis=-1, keepdims=True)
    second = jnp.mean(scaled * normed, axis=-1, keepdims=True)
    grad_in = inverse * (scaled - mean_grad - normed * second)
    lead_axes = tuple(range(upstream.ndim - 1))
    return (grad_in, jnp.sum(upstream * normed, axis=lead_axes), jnp.sum(upstream, axis=lead_axes))


def gelu_parts(hidden):
    normal_cdf = 0.5 * (1.0 + jax.scipy.special.erf(hidden * SQRT_HALF))
    density = jnp.exp(-0.5 * hidden * hidden) * INV_ROOT_TAU
    return (hidden * normal_cdf, normal_cdf + hidden * density)


def to_windows(field_in):
    num_rows, num_cols, width = field_in.shape
    pieces = field_in.reshape(num_rows // WS, WS, num_cols // WS, WS, width)
    return pieces.transpose(0, 2, 1, 3, 4).reshape(-1, WS * WS, width)


def from_windows(tiles, num_rows, num_cols):
    pieces = tiles.reshape(num_rows // WS, num_cols // WS, WS, WS, tiles.shape[-1])
    return pieces.transpose(0, 2, 1, 3, 4).reshape(num_rows, num_cols, tiles.shape[-1])


def make_mask(regions):
    num_rows, num_cols = regions.shape
    region_tiles = (
        regions.reshape(num_rows // WS, WS, num_cols // WS, WS)
        .transpose(0, 2, 1, 3)
        .reshape(-1, WS * WS)
    )
    same_region = region_tiles[..., :, None] == region_tiles[..., None, :]
    return jnp.where(same_region, 0.0, MASKED).astype(jnp.float32)


def one_hot_index(relative_index, entries):
    return (relative_index[..., None] == jnp.arange(entries, dtype=jnp.int32)).astype(jnp.bfloat16)


def table_bias(table_low, relative_index):
    onehot = one_hot_index(relative_index, table_low.shape[-1])
    return jnp.einsum("ijr,hr->hij", onehot, table_low, preferred_element_type=jnp.float32)


def table_grad(bias_grad, relative_index, entries):
    onehot = one_hot_index(relative_index, entries).astype(jnp.float32)
    return jnp.einsum("hij,ijr->hr", bias_grad, onehot, precision=lax.Precision.HIGHEST)


def split_heads(tiles, num_heads):
    return tiles.reshape(tiles.shape[0], tiles.shape[1], num_heads, -1).transpose(0, 2, 1, 3)


def join_heads(tiles):
    count, num_heads, positions, head_dim = tiles.shape
    return tiles.transpose(0, 2, 1, 3).reshape(count, positions, num_heads * head_dim)


def mm(form, left, right):
    return jnp.einsum(form, left, right, preferred_element_type=jnp.float32)


def reduce_kernel(sources, chunks, pairs, halves, *refs):
    count = len(chunks)
    columns = [pl.ds(start, width) for _, start, width in chunks]
    grads = [refs[at] for at, _, _ in chunks]
    outs = [refs[sources + at] for at, _, _ in chunks]
    rest = refs[2 * sources :]
    stages = [rest[at * count : (at + 1) * count] for at in range(7)]
    first_in, first_sum, second_in, second_sum, third_in, third_sum, fourth_in = stages
    send_sem, recv_sem = rest[7 * count :]
    place, line = lax.axis_index("fsdp"), lax.axis_index("seq")
    pair, core = place // 2, place % 2
    half, side = line // 2, line % 2
    mesh_id = pl.DeviceIdType.MESH

    def on_fsdp(pair_at, core_at):
        return {"fsdp": pair_at * 2 + core_at, "seq": line}

    def on_seq(half_at, side_at):
        return {"fsdp": place, "seq": half_at * 2 + side_at}

    pair_peers = [(pair + step) % pairs for step in range(1, pairs)]
    half_peers = [(half + step) % halves for step in range(1, halves)]
    everyone = [on_fsdp(pair, 1 - core)] + [on_fsdp(peer, core) for peer in pair_peers]
    everyone += [on_seq(half, 1 - side)] + [on_seq(peer, side) for peer in half_peers]
    barrier = pltpu.get_barrier_semaphore()
    for device in everyone:
        pl.semaphore_signal(barrier, inc=1, device_id=device, device_id_type=mesh_id)
    pl.semaphore_wait(barrier, len(everyone))

    started = {}
    used = [0] * count

    def send(stage, at, source, target, device):
        slot = used[at]
        used[at] += 1
        copy = pltpu.make_async_remote_copy(
            src_ref=source,
            dst_ref=target,
            send_sem=send_sem.at[at, slot],
            recv_sem=recv_sem.at[at, slot],
            device_id=device,
            device_id_type=mesh_id,
        )
        copy.start()
        started.setdefault((stage, at), []).append(copy)

    def arrived(stage, at):
        for copy in started[(stage, at)]:
            copy.wait_recv()

    def add(target, terms, low):
        total = terms[0].astype(jnp.float32)
        for term in terms[1:]:
            total = total + term.astype(jnp.float32)
        target[low] = total.astype(target.dtype)

    def sum_pair(at, pair_at):
        @pl.loop(0, 2 * halves)
        def _(piece):
            mine = grads[at][pair_at, core, piece // 2, piece % 2, :, columns[at]]
            came = first_in[at][pair_at, piece // 2, piece % 2]
            add(first_sum[at], [mine, came], (pair_at, piece // 2, piece % 2))

    def sum_side(at, side_at):
        @pl.loop(0, halves)
        def _(piece):
            terms = [first_sum[at][pair, piece, side_at]]
            terms += [second_in[at][step, piece, side_at] for step in range(pairs - 1)]
            add(second_sum[at], terms, (piece, side_at))

    def stage_first(at):
        send(0, at, grads[at].at[:, 1 - core, :, :, :, columns[at]], first_in[at], on_fsdp(pair, 1 - core))

    def stage_second(at):
        arrived(0, at)
        for step, peer in enumerate(pair_peers):
            sum_pair(at, peer)
            send(1, at, first_sum[at].at[peer], second_in[at].at[step], on_fsdp(peer, core))
        sum_pair(at, pair)

    def stage_third(at):
        arrived(1, at)
        sum_side(at, 1 - side)
        send(2, at, second_sum[at].at[:, 1 - side], third_in[at], on_seq(half, 1 - side))
        sum_side(at, side)

    def stage_fourth(at):
        arrived(2, at)

        @pl.loop(0, halves)
        def _(piece):
            add(third_sum[at], [second_sum[at][piece, side], third_in[at][piece]], (piece,))

        for step, peer in enumerate(half_peers):
            send(3, at, third_sum[at].at[peer], fourth_in[at].at[step], on_seq(peer, side))

    def stage_fifth(at):
        arrived(3, at)
        terms = [third_sum[at][half]] + [fourth_in[at][step] for step in range(halves - 1)]
        add(outs[at], terms, (half, side, slice(None), columns[at]))
        own = outs[at].at[half, side, :, columns[at]]
        for peer in half_peers:
            send(4, at, own, own, on_seq(peer, side))

    def stage_sixth(at):
        arrived(4, at)
        own = outs[at].at[:, side, :, columns[at]]
        send(5, at, own, own, on_seq(half, 1 - side))

    for at in range(count):
        stage_first(at)
    later = (stage_second, stage_third, stage_fourth, stage_fifth, stage_sixth)
    for tick in range(count + len(later) - 1):
        for lag, stage in enumerate(later):
            if 0 <= tick - lag < count:
                stage(tick - lag)
    for at in range(count):
        arrived(5, at)
    for copies in started.values():
        for copy in copies:
            copy.wait_send()


def reduce_all(grads, owners, size):
    pairs, halves, count = owners // 2, size // 2, len(grads)
    blocks, shapes = [], []
    for grad in grads:
        rows, columns = grad.shape[0] // (owners * size), grad.shape[1]
        if rows % 16:
            rows, columns = rows * columns // 128, 128
        shapes.append((rows, columns))
        blocks.append(grad.reshape(pairs, 2, halves, 2, rows, columns))
    leads = [
        (pairs, halves, 2),
        (pairs, halves, 2),
        (max(pairs - 1, 1), halves, 2),
        (halves, 2),
        (halves,),
        (halves,),
        (max(halves - 1, 1),),
    ]
    chunks = []
    for at, (rows, columns) in enumerate(shapes):
        parts = 2 if columns % 256 == 0 and grads[at].size > 2 * grads[-2].size else 1
        chunks += [(at, step * (columns // parts), columns // parts) for step in range(parts)]
    scratch = [
        pltpu.VMEM(lead + (shapes[at][0], width), jnp.bfloat16)
        for lead in leads
        for at, _, width in chunks
    ]
    copies = 3 + (pairs - 1) + 2 * (halves - 1)
    sems = [pltpu.SemaphoreType.DMA((len(chunks), copies))] * 2
    totals = pl.pallas_call(
        functools.partial(reduce_kernel, count, tuple(chunks), pairs, halves),
        out_shape=[jax.ShapeDtypeStruct((halves, 2) + shape, jnp.bfloat16) for shape in shapes],
        in_specs=[pl.BlockSpec(memory_space=pltpu.VMEM)] * count,
        out_specs=[pl.BlockSpec(memory_space=pltpu.VMEM)] * count,
        scratch_shapes=scratch + sems,
        compiler_params=pltpu.CompilerParams(collective_id=0, has_side_effects=True),
    )(*blocks)
    return [
        total.reshape(grad.shape[0] // owners, grad.shape[1]) for total, grad in zip(totals, grads)
    ]


def gather_kernel(count, pairs, *refs):
    shards_in, fulls = refs[:count], refs[count : 2 * count]
    send_sem, recv_sem, copy_sem = refs[2 * count :]
    place, line = lax.axis_index("fsdp"), lax.axis_index("seq")
    pair, core = place // 2, place % 2
    half, side = line // 2, line % 2
    mesh_id = pl.DeviceIdType.MESH
    partner = {"fsdp": pair * 2 + 1 - core, "seq": line}
    beside = {"fsdp": place, "seq": half * 2 + 1 - side}
    peers = [(pair + step) % pairs for step in range(1, pairs)]
    sources = [(pair + pairs - step) % pairs for step in range(1, pairs)]
    across = [{"fsdp": peer * 2 + core, "seq": line} for peer in peers]
    barrier = pltpu.get_barrier_semaphore()
    for device in [partner, beside] + across:
        pl.semaphore_signal(barrier, inc=1, device_id=device, device_id_type=mesh_id)
    pl.semaphore_wait(barrier, 2 + len(across))

    started = []

    def send(at, slot, source, target, device):
        copy = pltpu.make_async_remote_copy(
            src_ref=source,
            dst_ref=target,
            send_sem=send_sem.at[at, slot],
            recv_sem=recv_sem.at[at, slot],
            device_id=device,
            device_id_type=mesh_id,
        )
        copy.start()
        started.append(copy)
        return copy

    far, near, last, kept = {}, {}, [], []
    for at in range(count):
        mine = fulls[at].at[pair, core]
        for step, device in enumerate(across):
            target = fulls[at].at[pair, core, side]
            far[at, step] = send(at, 1 + 3 * step, shards_in[at].at[side], target, device)
        last.append(send(at, 0, shards_in[at], mine, partner))
        copy = pltpu.make_async_copy(shards_in[at], mine, copy_sem.at[at])
        copy.start()
        kept.append(copy)
    for tick in range(count + 1):
        if tick < count:
            for step, source in enumerate(sources):
                far[tick, step].wait_recv()
                came = fulls[tick].at[source, core, side]
                near[tick, step] = send(tick, 2 + 3 * step, came, came, beside)
        if tick:
            for step, source in enumerate(sources):
                near[tick - 1, step].wait_recv()
                came = fulls[tick - 1].at[source, core]
                last.append(send(tick - 1, 3 + 3 * step, came, came, partner))
    for copy in last:
        copy.wait_recv()
    for copy in kept:
        copy.wait()
    for copy in started:
        copy.wait_send()


def gather_all(weights, owners):
    pairs, count = owners // 2, len(weights)
    shards_in = [weight.reshape(2, weight.shape[0] // 2, weight.shape[1]) for weight in weights]
    copies = 1 + 3 * (pairs - 1)
    fulls = pl.pallas_call(
        functools.partial(gather_kernel, count, pairs),
        out_shape=[
            jax.ShapeDtypeStruct((pairs, 2) + shard.shape, shard.dtype) for shard in shards_in
        ],
        in_specs=[pl.BlockSpec(memory_space=pltpu.VMEM)] * count,
        out_specs=[pl.BlockSpec(memory_space=pltpu.VMEM)] * count,
        scratch_shapes=[pltpu.SemaphoreType.DMA((count, copies))] * 2
        + [pltpu.SemaphoreType.DMA((count,))],
        compiler_params=pltpu.CompilerParams(collective_id=1, has_side_effects=True),
    )(*shards_in)
    return [full.reshape(-1, full.shape[-1]) for full in fulls]


def shifted_rows(field, size):
    ring = [(at, (at - 1) % size) for at in range(size)]
    later = lax.ppermute(field[:SHIFT], "seq", ring)
    return jnp.roll(jnp.concatenate([field[SHIFT:], later], axis=0), -SHIFT, axis=1)


def unshifted_rows(field, size):
    ring = [(at, (at + 1) % size) for at in range(size)]
    field = jnp.roll(field, SHIFT, axis=1)
    keep = field.shape[0] - SHIFT
    earlier = lax.ppermute(field[keep:], "seq", ring)
    return jnp.concatenate([earlier, field[:keep]], axis=0)


def shards(
    tokens,
    cotangent,
    region_ids,
    relative_index,
    first_gain,
    first_offset,
    qkv_weight,
    proj_weight,
    bias_table,
    second_gain,
    second_offset,
    expand_weight,
    reduce_weight,
):
    owners = lax.axis_size("fsdp")
    size = lax.axis_size("seq")
    part = first_gain.shape[0]
    small = jnp.concatenate(
        [first_gain, first_offset, second_gain, second_offset, bias_table.reshape(-1)]
    )
    filled = jnp.pad(small, (0, -small.shape[0] % (32 * 128))).reshape(-1, 128)
    small_full, qkv_full, proj_full, expand_full, reduce_full = gather_all(
        [filled, qkv_weight, proj_weight, expand_weight, reduce_weight], owners
    )
    small_full = small_full.reshape(owners, -1)[:, : small.shape[0]]
    vectors = [
        small_full[:, at * part : (at + 1) * part].reshape(-1).astype(jnp.float32)
        for at in range(4)
    ]
    gain_one, offset_one, gain_two, offset_two = vectors
    table_rows, entries = bias_table.shape
    table_full = small_full[:, 4 * part :].reshape(-1, entries)
    _, num_rows, num_cols, width = tokens.shape
    num_heads = table_full.shape[0]
    query_scale = (width // num_heads) ** (-0.5)

    image_low = to_windows(shifted_rows(tokens[0], size))
    cot = to_windows(shifted_rows(cotangent[0], size))
    inputs = image_low.astype(jnp.float32)
    rel_bias = table_bias(table_full, relative_index)
    regions = lax.dynamic_slice_in_dim(
        region_ids, lax.axis_index("seq") * num_rows, num_rows, 0
    )
    mask_add = make_mask(regions)

    normed_one, hat_one, inv_one = layer_norm(inputs, gain_one, offset_one)
    first_low = normed_one.astype(jnp.bfloat16)
    factors = jnp.concatenate(
        [jnp.full((width,), query_scale, jnp.float32), jnp.ones((2 * width,), jnp.float32)]
    )
    qkv = (mm("wic,cd->wid", first_low, qkv_full) * factors).astype(jnp.bfloat16)
    queries = split_heads(qkv[..., :width], num_heads)
    keys = split_heads(qkv[..., width : 2 * width], num_heads)
    values = split_heads(qkv[..., 2 * width :], num_heads)
    scores = mm("whid,whjd->whij", queries, keys) + rel_bias + mask_add[:, None]
    exp_scores = jnp.exp(scores)
    row_total = jnp.sum(exp_scores, axis=-1, keepdims=True)
    probs = exp_scores / row_total
    probs_low = probs.astype(jnp.bfloat16)
    attended = join_heads(mm("whij,whjd->whid", probs_low, values).astype(jnp.bfloat16))

    middle = inputs + mm("wic,cd->wid", attended, proj_full)
    normed_two, hat_two, inv_two = layer_norm(middle, gain_two, offset_two)
    second_low = normed_two.astype(jnp.bfloat16)
    hidden = mm("wic,cf->wif", second_low, expand_full)
    activated, slope = gelu_parts(hidden)
    act_low = activated.astype(jnp.bfloat16)
    out_tiles = (middle + mm("wif,fc->wic", act_low, reduce_full)).astype(jnp.bfloat16)
    output = unshifted_rows(from_windows(out_tiles, num_rows, num_cols), size)[None]

    reduce_grad = mm("wif,wic->fc", act_low, cot)
    hidden_grad = (mm("wic,fc->wif", cot, reduce_full) * slope).astype(jnp.bfloat16)
    expand_grad = mm("wic,wif->cf", second_low, hidden_grad)
    upstream_two = mm("wif,cf->wic", hidden_grad, expand_full)
    back_two, gain_two_grad, offset_two_grad = norm_back(upstream_two, hat_two, inv_two, gain_two)
    middle_grad = cot.astype(jnp.float32) + back_two
    middle_low = middle_grad.astype(jnp.bfloat16)
    proj_grad = mm("wic,wid->cd", attended, middle_low)

    attended_grad = mm("wid,cd->wic", middle_low, proj_full).astype(jnp.bfloat16)
    grad_tiles = split_heads(attended_grad, num_heads)
    value_grad = mm("whij,whid->whjd", probs_low, grad_tiles)
    prob_grad = mm("whid,whjd->whij", grad_tiles, values)
    score_grad = probs * (prob_grad - jnp.sum(probs * prob_grad, axis=-1, keepdims=True))
    score_low = score_grad.astype(jnp.bfloat16)
    query_grad = mm("whij,whjd->whid", score_low, keys) * query_scale
    key_grad = mm("whij,whid->whjd", score_low, queries)
    qkv_grad = jnp.concatenate(
        [join_heads(grad.astype(jnp.bfloat16)) for grad in (query_grad, key_grad, value_grad)],
        axis=-1,
    )
    table_part = table_grad(jnp.sum(score_grad, axis=0), relative_index, entries)
    qkv_grad_w = mm("wic,wid->cd", first_low, qkv_grad)
    upstream_one = mm("wid,cd->wic", qkv_grad, qkv_full)
    back_one, gain_one_grad, offset_one_grad = norm_back(upstream_one, hat_one, inv_one, gain_one)
    grad_in = from_windows(middle_grad + back_one, num_rows, num_cols)
    tokens_grad = unshifted_rows(grad_in, size)[None]

    small_grads = jnp.concatenate(
        [
            grad.reshape(owners, -1)
            for grad in (gain_one_grad, offset_one_grad, gain_two_grad, offset_two_grad, table_part)
        ],
        axis=1,
    )
    step = size * 16 * 128
    extra = -small_grads.shape[1] % step
    small_grads = jnp.pad(small_grads, ((0, 0), (0, extra))).reshape(-1, 128)
    wanted = (expand_grad, reduce_grad, qkv_grad_w, proj_grad, small_grads)
    expand_total, reduce_total, qkv_total, proj_total, small_total = reduce_all(
        [grad.astype(jnp.bfloat16) for grad in wanted], owners, size
    )
    small_total = small_total.reshape(-1).astype(jnp.float32)
    own = [small_total[at * part : (at + 1) * part] for at in range(4)]
    table_total = small_total[4 * part : 4 * part + table_rows * entries].reshape(table_rows, entries)
    wide = jnp.float32
    return (
        output,
        tokens_grad,
        own[0],
        own[1],
        qkv_total.astype(wide),
        proj_total.astype(wide),
        table_total,
        own[2],
        own[3],
        expand_total.astype(wide),
        reduce_total.astype(wide),
    )


def solution(mesh):
    placed = (
        P("fsdp", "seq", None, None),
        P("fsdp", "seq", None, None),
        P(),
        P(),
        P("fsdp"),
        P("fsdp"),
        P("fsdp", None),
        P("fsdp", None),
        P("fsdp", None),
        P("fsdp"),
        P("fsdp"),
        P("fsdp", None),
        P("fsdp", None),
    )
    return jax.shard_map(
        shards,
        mesh=mesh,
        in_specs=placed,
        out_specs=(
            P("fsdp", "seq", None, None),
            P("fsdp", "seq", None, None),
            P("fsdp"),
            P("fsdp"),
            P("fsdp", None),
            P("fsdp", None),
            P("fsdp", None),
            P("fsdp"),
            P("fsdp"),
            P("fsdp", None),
            P("fsdp", None),
        ),
        check_vma=False,
    )
```

```python
import functools

import jax
import jax.numpy as jnp
from jax import lax
from jax.experimental import pallas as pl
from jax.experimental.pallas import tpu as pltpu
from jax.sharding import PartitionSpec as P

WS = 7
SHIFT = 3


EPSILON = 1e-05
MASKED = -100.0
SQRT_HALF = 0.7071067811865476
INV_ROOT_TAU = 0.3989422804014327


def layer_norm(values, norm_gain, norm_offset):
    average = jnp.mean(values, axis=-1, keepdims=True)
    centred = values - average
    variance = jnp.mean(centred * centred, axis=-1, keepdims=True)
    inverse = lax.rsqrt(variance + EPSILON)
    normed = centred * inverse
    return (normed * norm_gain + norm_offset, normed, inverse)


def norm_back(upstream, normed, inverse, norm_gain):
    scaled = upstream * norm_gain
    mean_grad = jnp.mean(scaled, axis=-1, keepdims=True)
    second = jnp.mean(scaled * normed, axis=-1, keepdims=True)
    grad_in = inverse * (scaled - mean_grad - normed * second)
    lead_axes = tuple(range(upstream.ndim - 1))
    return (grad_in, jnp.sum(upstream * normed, axis=lead_axes), jnp.sum(upstream, axis=lead_axes))


def gelu_parts(hidden):
    normal_cdf = 0.5 * (1.0 + jax.scipy.special.erf(hidden * SQRT_HALF))
    density = jnp.exp(-0.5 * hidden * hidden) * INV_ROOT_TAU
    return (hidden * normal_cdf, normal_cdf + hidden * density)


def to_windows(field_in):
    num_rows, num_cols, width = field_in.shape
    pieces = field_in.reshape(num_rows // WS, WS, num_cols // WS, WS, width)
    return pieces.transpose(0, 2, 1, 3, 4).reshape(-1, WS * WS, width)


def from_windows(tiles, num_rows, num_cols):
    pieces = tiles.reshape(num_rows // WS, num_cols // WS, WS, WS, tiles.shape[-1])
    return pieces.transpose(0, 2, 1, 3, 4).reshape(num_rows, num_cols, tiles.shape[-1])


def make_mask(regions):
    num_rows, num_cols = regions.shape
    region_tiles = (
        regions.reshape(num_rows // WS, WS, num_cols // WS, WS)
        .transpose(0, 2, 1, 3)
        .reshape(-1, WS * WS)
    )
    same_region = region_tiles[..., :, None] == region_tiles[..., None, :]
    return jnp.where(same_region, 0.0, MASKED).astype(jnp.float32)


def one_hot_index(relative_index, entries):
    return (relative_index[..., None] == jnp.arange(entries, dtype=jnp.int32)).astype(jnp.bfloat16)


def table_bias(table_low, relative_index):
    onehot = one_hot_index(relative_index, table_low.shape[-1])
    return jnp.einsum("ijr,hr->hij", onehot, table_low, preferred_element_type=jnp.float32)


def table_grad(bias_grad, relative_index, entries):
    onehot = one_hot_index(relative_index, entries).astype(jnp.float32)
    return jnp.einsum("hij,ijr->hr", bias_grad, onehot, precision=lax.Precision.HIGHEST)


def split_heads(tiles, num_heads):
    return tiles.reshape(tiles.shape[0], tiles.shape[1], num_heads, -1).transpose(0, 2, 1, 3)


def join_heads(tiles):
    count, num_heads, positions, head_dim = tiles.shape
    return tiles.transpose(0, 2, 1, 3).reshape(count, positions, num_heads * head_dim)


def mm(form, left, right):
    return jnp.einsum(form, left, right, preferred_element_type=jnp.float32)


def reduce_kernel(sources, chunks, pairs, halves, *refs):
    count = len(chunks)
    columns = [pl.ds(start, width) for _, start, width in chunks]
    grads = [refs[at] for at, _, _ in chunks]
    outs = [refs[sources + at] for at, _, _ in chunks]
    rest = refs[2 * sources :]
    stages = [rest[at * count : (at + 1) * count] for at in range(7)]
    first_in, first_sum, second_in, second_sum, third_in, third_sum, fourth_in = stages
    send_sem, recv_sem = rest[7 * count :]
    place, line = lax.axis_index("fsdp"), lax.axis_index("seq")
    pair, core = place // 2, place % 2
    half, side = line // 2, line % 2
    mesh_id = pl.DeviceIdType.MESH

    def on_fsdp(pair_at, core_at):
        return {"fsdp": pair_at * 2 + core_at, "seq": line}

    def on_seq(half_at, side_at):
        return {"fsdp": place, "seq": half_at * 2 + side_at}

    pair_peers = [(pair + step) % pairs for step in range(1, pairs)]
    half_peers = [(half + step) % halves for step in range(1, halves)]
    everyone = [on_fsdp(pair, 1 - core)] + [on_fsdp(peer, core) for peer in pair_peers]
    everyone += [on_seq(half, 1 - side)] + [on_seq(peer, side) for peer in half_peers]
    barrier = pltpu.get_barrier_semaphore()
    for device in everyone:
        pl.semaphore_signal(barrier, inc=1, device_id=device, device_id_type=mesh_id)
    pl.semaphore_wait(barrier, len(everyone))

    started = {}
    used = [0] * count

    def send(stage, at, source, target, device):
        slot = used[at]
        used[at] += 1
        copy = pltpu.make_async_remote_copy(
            src_ref=source,
            dst_ref=target,
            send_sem=send_sem.at[at, slot],
            recv_sem=recv_sem.at[at, slot],
            device_id=device,
            device_id_type=mesh_id,
        )
        copy.start()
        started.setdefault((stage, at), []).append(copy)

    def arrived(stage, at):
        for copy in started[(stage, at)]:
            copy.wait_recv()

    def add(target, terms, low):
        total = terms[0].astype(jnp.float32)
        for term in terms[1:]:
            total = total + term.astype(jnp.float32)
        target[low] = total.astype(target.dtype)

    def sum_pair(at, pair_at):
        @pl.loop(0, 2 * halves)
        def _(piece):
            mine = grads[at][pair_at, core, piece // 2, piece % 2, :, columns[at]]
            came = first_in[at][pair_at, piece // 2, piece % 2]
            add(first_sum[at], [mine, came], (pair_at, piece // 2, piece % 2))

    def sum_side(at, side_at):
        @pl.loop(0, halves)
        def _(piece):
            terms = [first_sum[at][pair, piece, side_at]]
            terms += [second_in[at][step, piece, side_at] for step in range(pairs - 1)]
            add(second_sum[at], terms, (piece, side_at))

    def stage_first(at):
        send(0, at, grads[at].at[:, 1 - core, :, :, :, columns[at]], first_in[at], on_fsdp(pair, 1 - core))

    def stage_second(at):
        arrived(0, at)
        for step, peer in enumerate(pair_peers):
            sum_pair(at, peer)
            send(1, at, first_sum[at].at[peer], second_in[at].at[step], on_fsdp(peer, core))
        sum_pair(at, pair)

    def stage_third(at):
        arrived(1, at)
        sum_side(at, 1 - side)
        send(2, at, second_sum[at].at[:, 1 - side], third_in[at], on_seq(half, 1 - side))
        sum_side(at, side)

    def stage_fourth(at):
        arrived(2, at)

        @pl.loop(0, halves)
        def _(piece):
            add(third_sum[at], [second_sum[at][piece, side], third_in[at][piece]], (piece,))

        for step, peer in enumerate(half_peers):
            send(3, at, third_sum[at].at[peer], fourth_in[at].at[step], on_seq(peer, side))

    def stage_fifth(at):
        arrived(3, at)
        terms = [third_sum[at][half]] + [fourth_in[at][step] for step in range(halves - 1)]
        add(outs[at], terms, (half, side, slice(None), columns[at]))
        own = outs[at].at[half, side, :, columns[at]]
        for peer in half_peers:
            send(4, at, own, own, on_seq(peer, side))

    def stage_sixth(at):
        arrived(4, at)
        own = outs[at].at[:, side, :, columns[at]]
        send(5, at, own, own, on_seq(half, 1 - side))

    for at in range(count):
        stage_first(at)
    later = (stage_second, stage_third, stage_fourth, stage_fifth, stage_sixth)
    for tick in range(count + 2 * (len(later) - 1)):
        for lag, stage in enumerate(later):
            if 0 <= tick - 2 * lag < count:
                stage(tick - 2 * lag)
    for at in range(count):
        arrived(5, at)
    for copies in started.values():
        for copy in copies:
            copy.wait_send()


def reduce_all(grads, owners, size):
    pairs, halves, count = owners // 2, size // 2, len(grads)
    blocks, shapes = [], []
    for grad in grads:
        rows, columns = grad.shape[0] // (owners * size), grad.shape[1]
        if rows % 16:
            rows, columns = rows * columns // 128, 128
        shapes.append((rows, columns))
        blocks.append(grad.reshape(pairs, 2, halves, 2, rows, columns))
    leads = [
        (pairs, halves, 2),
        (pairs, halves, 2),
        (max(pairs - 1, 1), halves, 2),
        (halves, 2),
        (halves,),
        (halves,),
        (max(halves - 1, 1),),
    ]
    chunks = []
    for at, (rows, columns) in enumerate(shapes):
        parts = 4 if columns % 512 == 0 and grads[at].size > 2 * grads[-2].size else 1
        chunks += [(at, step * (columns // parts), columns // parts) for step in range(parts)]
    scratch = [
        pltpu.VMEM(lead + (shapes[at][0], width), jnp.bfloat16)
        for lead in leads
        for at, _, width in chunks
    ]
    copies = 3 + (pairs - 1) + 2 * (halves - 1)
    sems = [pltpu.SemaphoreType.DMA((len(chunks), copies))] * 2
    totals = pl.pallas_call(
        functools.partial(reduce_kernel, count, tuple(chunks), pairs, halves),
        out_shape=[jax.ShapeDtypeStruct((halves, 2) + shape, jnp.bfloat16) for shape in shapes],
        in_specs=[pl.BlockSpec(memory_space=pltpu.VMEM)] * count,
        out_specs=[pl.BlockSpec(memory_space=pltpu.VMEM)] * count,
        scratch_shapes=scratch + sems,
        compiler_params=pltpu.CompilerParams(collective_id=0, has_side_effects=True),
    )(*blocks)
    return [
        total.reshape(grad.shape[0] // owners, grad.shape[1]) for total, grad in zip(totals, grads)
    ]


def gather_kernel(count, pairs, *refs):
    shards_in, fulls = refs[:count], refs[count : 2 * count]
    send_sem, recv_sem, copy_sem = refs[2 * count :]
    place, line = lax.axis_index("fsdp"), lax.axis_index("seq")
    pair, core = place // 2, place % 2
    half, side = line // 2, line % 2
    mesh_id = pl.DeviceIdType.MESH
    partner = {"fsdp": pair * 2 + 1 - core, "seq": line}
    beside = {"fsdp": place, "seq": half * 2 + 1 - side}
    peers = [(pair + step) % pairs for step in range(1, pairs)]
    sources = [(pair + pairs - step) % pairs for step in range(1, pairs)]
    across = [{"fsdp": peer * 2 + core, "seq": line} for peer in peers]
    barrier = pltpu.get_barrier_semaphore()
    for device in [partner, beside] + across:
        pl.semaphore_signal(barrier, inc=1, device_id=device, device_id_type=mesh_id)
    pl.semaphore_wait(barrier, 2 + len(across))

    started = []

    def send(at, slot, source, target, device):
        copy = pltpu.make_async_remote_copy(
            src_ref=source,
            dst_ref=target,
            send_sem=send_sem.at[at, slot],
            recv_sem=recv_sem.at[at, slot],
            device_id=device,
            device_id_type=mesh_id,
        )
        copy.start()
        started.append(copy)
        return copy

    far, near, last, kept = {}, {}, [], []
    for at in range(count):
        mine = fulls[at].at[pair, core]
        for step, device in enumerate(across):
            target = fulls[at].at[pair, core, side]
            far[at, step] = send(at, 1 + 3 * step, shards_in[at].at[side], target, device)
        last.append(send(at, 0, shards_in[at], mine, partner))
        copy = pltpu.make_async_copy(shards_in[at], mine, copy_sem.at[at])
        copy.start()
        kept.append(copy)
    for tick in range(count + 1):
        if tick < count:
            for step, source in enumerate(sources):
                far[tick, step].wait_recv()
                came = fulls[tick].at[source, core, side]
                near[tick, step] = send(tick, 2 + 3 * step, came, came, beside)
        if tick:
            for step, source in enumerate(sources):
                near[tick - 1, step].wait_recv()
                came = fulls[tick - 1].at[source, core]
                last.append(send(tick - 1, 3 + 3 * step, came, came, partner))
    for copy in last:
        copy.wait_recv()
    for copy in kept:
        copy.wait()
    for copy in started:
        copy.wait_send()


def gather_all(weights, owners):
    pairs, count = owners // 2, len(weights)
    shards_in = [weight.reshape(2, weight.shape[0] // 2, weight.shape[1]) for weight in weights]
    copies = 1 + 3 * (pairs - 1)
    fulls = pl.pallas_call(
        functools.partial(gather_kernel, count, pairs),
        out_shape=[
            jax.ShapeDtypeStruct((pairs, 2) + shard.shape, shard.dtype) for shard in shards_in
        ],
        in_specs=[pl.BlockSpec(memory_space=pltpu.VMEM)] * count,
        out_specs=[pl.BlockSpec(memory_space=pltpu.VMEM)] * count,
        scratch_shapes=[pltpu.SemaphoreType.DMA((count, copies))] * 2
        + [pltpu.SemaphoreType.DMA((count,))],
        compiler_params=pltpu.CompilerParams(collective_id=1, has_side_effects=True),
    )(*shards_in)
    return [full.reshape(-1, full.shape[-1]) for full in fulls]


def shifted_rows(field, size):
    ring = [(at, (at - 1) % size) for at in range(size)]
    later = lax.ppermute(field[:SHIFT], "seq", ring)
    return jnp.roll(jnp.concatenate([field[SHIFT:], later], axis=0), -SHIFT, axis=1)


def unshifted_rows(field, size):
    ring = [(at, (at + 1) % size) for at in range(size)]
    field = jnp.roll(field, SHIFT, axis=1)
    keep = field.shape[0] - SHIFT
    earlier = lax.ppermute(field[keep:], "seq", ring)
    return jnp.concatenate([earlier, field[:keep]], axis=0)


def shards(
    tokens,
    cotangent,
    region_ids,
    relative_index,
    first_gain,
    first_offset,
    qkv_weight,
    proj_weight,
    bias_table,
    second_gain,
    second_offset,
    expand_weight,
    reduce_weight,
):
    owners = lax.axis_size("fsdp")
    size = lax.axis_size("seq")
    part = first_gain.shape[0]
    small = jnp.concatenate(
        [first_gain, first_offset, second_gain, second_offset, bias_table.reshape(-1)]
    )
    filled = jnp.pad(small, (0, -small.shape[0] % (32 * 128))).reshape(-1, 128)
    expand_full, reduce_full, qkv_full, proj_full, small_full = gather_all(
        [expand_weight, reduce_weight, qkv_weight, proj_weight, filled], owners
    )
    small_full = small_full.reshape(owners, -1)[:, : small.shape[0]]
    vectors = [
        small_full[:, at * part : (at + 1) * part].reshape(-1).astype(jnp.float32)
        for at in range(4)
    ]
    gain_one, offset_one, gain_two, offset_two = vectors
    table_rows, entries = bias_table.shape
    table_full = small_full[:, 4 * part :].reshape(-1, entries)
    _, num_rows, num_cols, width = tokens.shape
    num_heads = table_full.shape[0]
    query_scale = (width // num_heads) ** (-0.5)

    image_low = to_windows(shifted_rows(tokens[0], size))
    cot = to_windows(shifted_rows(cotangent[0], size))
    inputs = image_low.astype(jnp.float32)
    rel_bias = table_bias(table_full, relative_index)
    regions = lax.dynamic_slice_in_dim(
        region_ids, lax.axis_index("seq") * num_rows, num_rows, 0
    )
    mask_add = make_mask(regions)

    normed_one, hat_one, inv_one = layer_norm(inputs, gain_one, offset_one)
    first_low = normed_one.astype(jnp.bfloat16)
    factors = jnp.concatenate(
        [jnp.full((width,), query_scale, jnp.float32), jnp.ones((2 * width,), jnp.float32)]
    )
    qkv = (mm("wic,cd->wid", first_low, qkv_full) * factors).astype(jnp.bfloat16)
    queries = split_heads(qkv[..., :width], num_heads)
    keys = split_heads(qkv[..., width : 2 * width], num_heads)
    values = split_heads(qkv[..., 2 * width :], num_heads)
    scores = mm("whid,whjd->whij", queries, keys) + rel_bias + mask_add[:, None]
    exp_scores = jnp.exp(scores)
    row_total = jnp.sum(exp_scores, axis=-1, keepdims=True)
    probs = exp_scores / row_total
    probs_low = probs.astype(jnp.bfloat16)
    attended = join_heads(mm("whij,whjd->whid", probs_low, values).astype(jnp.bfloat16))

    middle = inputs + mm("wic,cd->wid", attended, proj_full)
    normed_two, hat_two, inv_two = layer_norm(middle, gain_two, offset_two)
    second_low = normed_two.astype(jnp.bfloat16)
    hidden = mm("wic,cf->wif", second_low, expand_full)
    activated, slope = gelu_parts(hidden)
    act_low = activated.astype(jnp.bfloat16)
    out_tiles = (middle + mm("wif,fc->wic", act_low, reduce_full)).astype(jnp.bfloat16)
    output = unshifted_rows(from_windows(out_tiles, num_rows, num_cols), size)[None]

    reduce_grad = mm("wif,wic->fc", act_low, cot)
    hidden_grad = (mm("wic,fc->wif", cot, reduce_full) * slope).astype(jnp.bfloat16)
    expand_grad = mm("wic,wif->cf", second_low, hidden_grad)
    upstream_two = mm("wif,cf->wic", hidden_grad, expand_full)
    back_two, gain_two_grad, offset_two_grad = norm_back(upstream_two, hat_two, inv_two, gain_two)
    middle_grad = cot.astype(jnp.float32) + back_two
    middle_low = middle_grad.astype(jnp.bfloat16)
    proj_grad = mm("wic,wid->cd", attended, middle_low)

    attended_grad = mm("wid,cd->wic", middle_low, proj_full).astype(jnp.bfloat16)
    grad_tiles = split_heads(attended_grad, num_heads)
    value_grad = mm("whij,whid->whjd", probs_low, grad_tiles)
    prob_grad = mm("whid,whjd->whij", grad_tiles, values)
    score_grad = probs * (prob_grad - jnp.sum(probs * prob_grad, axis=-1, keepdims=True))
    score_low = score_grad.astype(jnp.bfloat16)
    query_grad = mm("whij,whjd->whid", score_low, keys) * query_scale
    key_grad = mm("whij,whid->whjd", score_low, queries)
    qkv_grad = jnp.concatenate(
        [join_heads(grad.astype(jnp.bfloat16)) for grad in (query_grad, key_grad, value_grad)],
        axis=-1,
    )
    table_part = table_grad(jnp.sum(score_grad, axis=0), relative_index, entries)
    qkv_grad_w = mm("wic,wid->cd", first_low, qkv_grad)
    upstream_one = mm("wid,cd->wic", qkv_grad, qkv_full)
    back_one, gain_one_grad, offset_one_grad = norm_back(upstream_one, hat_one, inv_one, gain_one)
    grad_in = from_windows(middle_grad + back_one, num_rows, num_cols)
    tokens_grad = unshifted_rows(grad_in, size)[None]

    small_grads = jnp.concatenate(
        [
            grad.reshape(owners, -1)
            for grad in (gain_one_grad, offset_one_grad, gain_two_grad, offset_two_grad, table_part)
        ],
        axis=1,
    )
    step = size * 16 * 128
    extra = -small_grads.shape[1] % step
    small_grads = jnp.pad(small_grads, ((0, 0), (0, extra))).reshape(-1, 128)
    wanted = (expand_grad, reduce_grad, qkv_grad_w, proj_grad, small_grads)
    expand_total, reduce_total, qkv_total, proj_total, small_total = reduce_all(
        [grad.astype(jnp.bfloat16) for grad in wanted], owners, size
    )
    small_total = small_total.reshape(-1).astype(jnp.float32)
    own = [small_total[at * part : (at + 1) * part] for at in range(4)]
    table_total = small_total[4 * part : 4 * part + table_rows * entries].reshape(table_rows, entries)
    wide = jnp.float32
    return (
        output,
        tokens_grad,
        own[0],
        own[1],
        qkv_total.astype(wide),
        proj_total.astype(wide),
        table_total,
        own[2],
        own[3],
        expand_total.astype(wide),
        reduce_total.astype(wide),
    )


def solution(mesh):
    placed = (
        P("fsdp", "seq", None, None),
        P("fsdp", "seq", None, None),
        P(),
        P(),
        P("fsdp"),
        P("fsdp"),
        P("fsdp", None),
        P("fsdp", None),
        P("fsdp", None),
        P("fsdp"),
        P("fsdp"),
        P("fsdp", None),
        P("fsdp", None),
    )
    return jax.shard_map(
        shards,
        mesh=mesh,
        in_specs=placed,
        out_specs=(
            P("fsdp", "seq", None, None),
            P("fsdp", "seq", None, None),
            P("fsdp"),
            P("fsdp"),
            P("fsdp", None),
            P("fsdp", None),
            P("fsdp", None),
            P("fsdp"),
            P("fsdp"),
            P("fsdp", None),
            P("fsdp", None),
        ),
        check_vma=False,
    )
```
